32 devices in a mesh: dp: 8 (over z, y), tensor: 4 (over x, core).
Axes of the slice: x: 2, y: 2, z: 4, core: 2. Of those that a mesh axis runs over, the one named last changes fastest.
Arguments:
- layer_input: bfloat16 [32, 197, 768], P('dp'), may hold values from -6 to 6
- group_images: int32 [8], P('dp'), may hold values from 1 to 4, as said below
- ln1_gain: float32 [768], replicated, may hold values from 0.25 to 1.75
- ln1_bias: float32 [768], replicated, may hold values from -1.75 to 1.75
- w_qkv: bfloat16 [768, 3, 768], P(None, None, 'tensor'), may hold values from -2 to 2
- bias_qv: float32 [768, 2], P('tensor'), may hold values from -3 to 3
- w_out: bfloat16 [768, 768], P(None, 'tensor'), may hold values from -0.625 to 0.625
- bias_out: float32 [768], replicated, may hold values from -1.75 to 1.75
- ln2_gain: float32 [768], replicated, may hold values from 0.25 to 1.75
- ln2_bias: float32 [768], replicated, may hold values from -1.75 to 1.75
- w_up: bfloat16 [768, 3072], P(None, 'tensor'), may hold values from -0.21875 to 0.21875
- bias_up: float32 [3072], P('tensor'), may hold values from -3 to 3
- w_down: bfloat16 [768, 3072], P(None, 'tensor'), may hold values from -0.15625 to 0.15625
- bias_down: float32 [768], replicated, may hold values from -1.75 to 1.75
- grad_out: bfloat16 [32, 197, 768], P('dp'), may hold values from -6 to 6
Outputs:
- output: bfloat16 [32, 197, 768], P('dp')
- grad_input: bfloat16 [32, 197, 768], P('dp')
- grad_ln1_gain: float32 [768], P('dp')
- grad_ln1_bias: float32 [768], P('dp')
- grad_w_qkv: float32 [768, 3, 768], P('dp', None, 'tensor')
- grad_bias_qv: float32 [768, 2], P(('tensor', 'dp'))
- grad_w_out: float32 [768, 768], P('dp', 'tensor')
- grad_bias_out: float32 [768], P('dp')
- grad_ln2_gain: float32 [768], P('dp')
- grad_ln2_bias: float32 [768], P('dp')
- grad_w_up: float32 [768, 3072], P('dp', 'tensor')
- grad_bias_up: float32 [3072], P(('tensor', 'dp'))
- grad_w_down: float32 [768, 3072], P('dp', 'tensor')
- grad_bias_down: float32 [768], P('dp')
The draws below stay inside these ranges and needn't reach their ends.
Inputs may be any that keep to these rules, and one draw needn't show every extreme that they name: Group g has live images in its first group_images[g] slots; in every draw some group is full.
All inputs are finite; a program needn't handle non-finite values.
Results may differ from the reference program's by a relative error of at most 0.019.
Values may be sent and summed in bfloat16 or wider, within the bound.
No kernel may reach another device: no remote copies, remote signals or barrier semaphores. Data moves between devices by JAX's collectives and lax.ppermute only.
A program may use at most 128 MiB of HBM per device.

```python
import math
import jax
import jax.numpy as jnp
from jax import lax

D = 768
HEADS = 12
HD = 64
FF = 3072
SEQ = 197
IMG_DEV = 4
GROUPS = 8
SLOTS = 32
N_TENSOR = 4


def draw_group_images(key, part):
    counts = jax.random.randint(key, (GROUPS,), 1, IMG_DEV + 1, dtype=jnp.int32)
    fullest = jax.random.randint(jax.random.fold_in(key, 3), (), 0, GROUPS, dtype=jnp.int32)
    return jnp.where(jnp.arange(GROUPS, dtype=jnp.int32) == fullest, IMG_DEV, counts).astype(jnp.int32)


def draw_w_qkv(key, part):
    normal_draw = jax.random.normal(key, (D, 3, D), jnp.float32) * D ** (-0.5)
    return normal_draw.astype(jnp.bfloat16)


def spiked(drawn, own_key, source, target, blocks, factor):
    owner, partner = [(jnp.arange(drawn.shape[dim]) // (drawn.shape[dim] // blocks)).reshape([-1 if axis == dim else 1 for axis in range(drawn.ndim)]) for dim in (source, target)]
    chosen = jax.random.permutation(own_key, blocks)[partner]
    strong = (owner == chosen) | (owner == (partner + blocks // 2) % blocks)
    return jnp.where(strong, factor * drawn, drawn)


def block_levels(rng, dims, split, smallest, largest):
    def one(axis_at, parts):
        draws = jax.random.uniform(jax.random.fold_in(jax.random.fold_in(rng, 6), axis_at), (parts,), jnp.float32, smallest / len(split), largest / len(split))
        return jnp.repeat(jnp.exp(draws), dims[axis_at] // parts).reshape((-1,) + (1,) * (len(dims) - axis_at - 1))

    loudness = one(*split[0])
    for cut in split[1:]:
        loudness = loudness * one(*cut)
    return loudness


def normal_values(rng, shape, spread, bound, shards=(), kind=jnp.bfloat16):
    loudness = block_levels(rng, shape, shards, -0.22, 0.18) if shards else 1.0
    result = jax.random.normal(rng, shape, jnp.float32) * spread * loudness
    return jnp.minimum(jnp.maximum(result, -bound), bound).astype(kind)


def heavy_noise(rng, dims, spread, limit, shards, heavy, kind=jnp.bfloat16):
    result = spread * jax.random.normal(rng, dims, jnp.float32)
    if shards:
        result = result * block_levels(rng, dims, shards, -0.22, 0.18)
    return jnp.clip(spiked(result, jax.random.fold_in(rng, 3), *heavy), -limit, limit).astype(kind)


def setup_inputs(seed: int = 0) -> dict:
    arg_keys = jax.random.split(jax.random.key(seed), 16)
    return {
        "layer_input": normal_values(arg_keys[0], (SLOTS, SEQ, D), 1.0, 6.0, ((0, 8),)),
        "group_images": draw_group_images(jax.random.fold_in(arg_keys[15], 71), 0),
        "ln1_gain": jnp.clip(1.0 + 0.15 * jax.random.normal(arg_keys[2], (D,), jnp.float32), 0.25, 1.75),
        "ln1_bias": normal_values(arg_keys[3], (D,), 0.3, 1.75, (), jnp.float32),
        "w_qkv": draw_w_qkv(jax.random.fold_in(arg_keys[15], 71), 0),
        "bias_qv": normal_values(arg_keys[5], (D, 2), 0.5, 3.0, ((0, 4),), jnp.float32),
        "w_out": normal_values(arg_keys[6], (D, D), (D // 8) ** -0.5, 0.625, ((1, 4),)),
        "bias_out": normal_values(arg_keys[7], (D,), 0.3, 1.75, (), jnp.float32),
        "ln2_gain": jnp.clip(1.0 + 0.15 * jax.random.normal(arg_keys[8], (D,), jnp.float32), 0.25, 1.75),
        "ln2_bias": normal_values(arg_keys[9], (D,), 0.3, 1.75, (), jnp.float32),
        "w_up": normal_values(arg_keys[10], (D, FF), D ** -0.5, 0.21875, ((1, 4),)),
        "bias_up": normal_values(arg_keys[11], (FF,), 0.5, 3.0, ((0, 4),), jnp.float32),
        "w_down": normal_values(arg_keys[12], (D, FF), (FF // 2) ** -0.5, 0.15625, ((1, 4),)),
        "bias_down": normal_values(arg_keys[13], (D,), 0.3, 1.75, (), jnp.float32),
        "grad_out": heavy_noise(arg_keys[14], (SLOTS, SEQ, D), 1.0, 6.0, ((0, 8),), (0, 2, 8, 2.0)),
    }


EPS = 1e-06
SQRT_HALF = 0.5 ** 0.5
INV_ROOT_TWO_PI = (0.5 / math.pi) ** 0.5

def norm_stats(values):
    row_mean = lax.optimization_barrier(jnp.mean(values, axis=-1, keepdims=True))
    centred = values - row_mean
    variance = lax.optimization_barrier(jnp.mean(centred * centred, axis=-1, keepdims=True))
    inverse = lax.rsqrt(variance + EPS)
    return (centred * inverse, inverse)

def norm_back(grad_norm, gain, normed, inverse):
    scaled = grad_norm * gain
    return inverse * (scaled - lax.optimization_barrier(jnp.mean(scaled, axis=-1, keepdims=True)) - normed * lax.optimization_barrier(jnp.mean(scaled * normed, axis=-1, keepdims=True)))

def gelu_value(pre):
    return 0.5 * pre * (1.0 + lax.erf(pre * SQRT_HALF))

def gelu_slope(pre):
    return 0.5 * (1.0 + lax.erf(pre * SQRT_HALF)) + pre * jnp.exp(-0.5 * pre * pre) * INV_ROOT_TWO_PI

def split_sum(pieces):
    running = None
    for left_side, right_side in pieces:
        partial_value = jnp.einsum('tk,mk->tm', left_side.astype(jnp.float32), right_side.astype(jnp.float32))
        rounded = lax.optimization_barrier(partial_value.astype(jnp.bfloat16)).astype(jnp.float32)
        running = rounded if running is None else running + rounded
    return running

def reference(layer_input, group_images, ln1_gain, ln1_bias, w_qkv, bias_qv, w_out, bias_out, ln2_gain, ln2_bias, w_up, bias_up, w_down, bias_down, grad_out):
    slot_count = layer_input.shape[0]
    block_size = math.gcd(slot_count, 16)
    slot_ids = jnp.arange(slot_count, dtype=jnp.int32)
    live_slots = (slot_ids % IMG_DEV < group_images[slot_ids // IMG_DEV]).astype(jnp.float32)
    score_scale = HD ** (-0.5)
    head_cols = D // N_TENSOR
    unit_cols = FF // N_TENSOR

    def one_block(running, inputs):
        block_input, block_grad, block_live = inputs
        image_count = block_input.shape[0]
        token_count = image_count * SEQ
        input_rows = block_input.reshape(token_count, D).astype(jnp.float32)
        live_rows = jnp.repeat(block_live, SEQ)[:, None]
        normed1, inverse1 = norm_stats(input_rows)
        norm_first = (normed1 * ln1_gain + ln1_bias).astype(jnp.bfloat16)
        qkv = jnp.einsum('td,dcj->tcj', norm_first.astype(jnp.float32), w_qkv.astype(jnp.float32))
        queries = (qkv[:, 0] + bias_qv[:, 0]).astype(jnp.bfloat16)
        key_rows = qkv[:, 1].astype(jnp.bfloat16)
        values = (qkv[:, 2] + bias_qv[:, 1]).astype(jnp.bfloat16)
        head_shape = (image_count, SEQ, HEADS, HD)
        query_heads = queries.reshape(head_shape).astype(jnp.float32)
        key_heads = key_rows.reshape(head_shape).astype(jnp.float32)
        value_heads = values.reshape(head_shape).astype(jnp.float32)
        scores = jnp.einsum('bqhe,bkhe->bhqk', query_heads, key_heads) * score_scale
        log_total = jax.nn.logsumexp(scores, axis=-1, keepdims=True)
        probs32 = jnp.exp(scores - log_total)
        probs = probs32.astype(jnp.bfloat16)
        mixed = jnp.einsum('bhqk,bkhe->bqhe', probs.astype(jnp.float32), value_heads).astype(jnp.bfloat16).reshape(token_count, D)
        proj = split_sum([(mixed[:, shard_index * head_cols:(shard_index + 1) * head_cols], w_out[:, shard_index * head_cols:(shard_index + 1) * head_cols]) for shard_index in range(N_TENSOR)])
        resid = input_rows + proj + bias_out
        normed2, inverse2 = norm_stats(resid)
        norm_second = (normed2 * ln2_gain + ln2_bias).astype(jnp.bfloat16)
        upper = jnp.dot(norm_second, w_up, preferred_element_type=jnp.float32) + bias_up
        activ = gelu_value(upper).astype(jnp.bfloat16)
        down_proj = split_sum([(activ[:, shard_index * unit_cols:(shard_index + 1) * unit_cols], w_down[:, shard_index * unit_cols:(shard_index + 1) * unit_cols]) for shard_index in range(N_TENSOR)])
        output_rows = (live_rows * (resid + down_proj + bias_down)).astype(jnp.bfloat16)
        grad_rows = (live_rows * block_grad.reshape(token_count, D).astype(jnp.float32)).astype(jnp.bfloat16)
        grad_rows32 = grad_rows.astype(jnp.float32)
        grad_w_down = jnp.dot(grad_rows32.T, activ.astype(jnp.float32))
        grad_bias_down = lax.optimization_barrier(jnp.sum(grad_rows32, axis=0))
        grad_upper = jnp.dot(grad_rows, w_down, preferred_element_type=jnp.float32) * gelu_slope(upper)
        grad_upper_b = grad_upper.astype(jnp.bfloat16)
        grad_w_up = jnp.dot(norm_second.astype(jnp.float32).T, grad_upper_b.astype(jnp.float32))
        grad_bias_up = lax.optimization_barrier(jnp.sum(grad_upper, axis=0))
        grad_norm2 = split_sum([(grad_upper_b[:, shard_index * unit_cols:(shard_index + 1) * unit_cols], w_up[:, shard_index * unit_cols:(shard_index + 1) * unit_cols]) for shard_index in range(N_TENSOR)])
        grad_ln2_gain = lax.optimization_barrier(jnp.sum(grad_norm2 * normed2, axis=0))
        grad_ln2_bias = lax.optimization_barrier(jnp.sum(grad_norm2, axis=0))
        grad_resid = grad_rows32 + norm_back(grad_norm2, ln2_gain, normed2, inverse2)
        grad_bias_out = lax.optimization_barrier(jnp.sum(grad_resid, axis=0))
        grad_resid_b = grad_resid.astype(jnp.bfloat16)
        grad_w_out = jnp.dot(grad_resid_b.astype(jnp.float32).T, mixed.astype(jnp.float32))
        grad_mixed = jnp.dot(grad_resid_b, w_out, preferred_element_type=jnp.float32).astype(jnp.bfloat16)
        grad_mixed_heads = grad_mixed.reshape(head_shape).astype(jnp.float32)
        grad_probs = jnp.einsum('bqhe,bkhe->bhqk', grad_mixed_heads, value_heads)
        delta = lax.optimization_barrier(jnp.sum(probs32 * grad_probs, axis=-1, keepdims=True))
        grad_scores = (probs32 * (grad_probs - delta) * score_scale).astype(jnp.bfloat16).astype(jnp.float32)
        grad_q32 = jnp.einsum('bhqk,bkhe->bqhe', grad_scores, key_heads).reshape(token_count, D)
        grad_k32 = jnp.einsum('bhqk,bqhe->bkhe', grad_scores, query_heads).reshape(token_count, D)
        grad_v32 = jnp.einsum('bhqk,bqhe->bkhe', probs.astype(jnp.float32), grad_mixed_heads).reshape(token_count, D)
        grad_qkv = jnp.stack([grad_q32.astype(jnp.bfloat16), grad_k32.astype(jnp.bfloat16), grad_v32.astype(jnp.bfloat16)], axis=1)
        grad_w_qkv = jnp.einsum('td,tcj->dcj', norm_first.astype(jnp.float32), grad_qkv.astype(jnp.float32))
        grad_bias_qv = jnp.stack([lax.optimization_barrier(jnp.sum(grad_q32, axis=0)), lax.optimization_barrier(jnp.sum(grad_v32, axis=0))], axis=1)
        grad_norm1 = split_sum([(grad_qkv[:, :, shard_index * head_cols:(shard_index + 1) * head_cols].reshape(token_count, 3 * head_cols), w_qkv[:, :, shard_index * head_cols:(shard_index + 1) * head_cols].reshape(D, 3 * head_cols)) for shard_index in range(N_TENSOR)])
        grad_ln1_gain = lax.optimization_barrier(jnp.sum(grad_norm1 * normed1, axis=0))
        grad_ln1_bias = lax.optimization_barrier(jnp.sum(grad_norm1, axis=0))
        grad_in_rows = (grad_resid + norm_back(grad_norm1, ln1_gain, normed1, inverse1)).astype(jnp.bfloat16)
        terms = (grad_ln1_gain, grad_ln1_bias, grad_w_qkv, grad_bias_qv, grad_w_out, grad_bias_out, grad_ln2_gain, grad_ln2_bias, grad_w_up, grad_bias_up, grad_w_down, grad_bias_down)
        running = jax.tree.map(jnp.add, running, terms)
        return (running, (output_rows.reshape(image_count, SEQ, D), grad_in_rows.reshape(image_count, SEQ, D)))
    initial = (jnp.zeros((D,), jnp.float32), jnp.zeros((D,), jnp.float32), jnp.zeros((D, 3, D), jnp.float32), jnp.zeros((D, 2), jnp.float32), jnp.zeros((D, D), jnp.float32), jnp.zeros((D,), jnp.float32), jnp.zeros((D,), jnp.float32), jnp.zeros((D,), jnp.float32), jnp.zeros((D, FF), jnp.float32), jnp.zeros((FF,), jnp.float32), jnp.zeros((D, FF), jnp.float32), jnp.zeros((D,), jnp.float32))
    block_count = slot_count // block_size
    sums, (outputs, grads) = lax.scan(one_block, initial, (layer_input.reshape(block_count, block_size, SEQ, D), grad_out.reshape(block_count, block_size, SEQ, D), live_slots.reshape(block_count, block_size)))
    output = outputs.reshape(slot_count, SEQ, D)
    grad_input = grads.reshape(slot_count, SEQ, D)
    return (output, grad_input, sums[0], sums[1], sums[2], sums[3], sums[4], sums[5], sums[6], sums[7], sums[8], sums[9], sums[10], sums[11])
```

```python
import functools
import math

import jax
import jax.numpy as jnp
from jax import lax
from jax.experimental import pallas as pl
from jax.experimental.pallas import tpu as pltpu
from jax.sharding import PartitionSpec as P

HD = 64
EPS = 1e-06
SQRT_HALF = 0.5**0.5
INV_ROOT_TWO_PI = (0.5 / math.pi) ** 0.5
F32 = jnp.float32
BF16 = jnp.bfloat16


def norm_stats(values):
    row_mean = jnp.mean(values, axis=-1, keepdims=True)
    centred = values - row_mean
    variance = jnp.mean(centred * centred, axis=-1, keepdims=True)
    inverse = lax.rsqrt(variance + EPS)
    return (centred * inverse, inverse)


def norm_back(grad_norm, gain, normed, inverse):
    scaled = grad_norm * gain
    return inverse * (
        scaled
        - jnp.mean(scaled, axis=-1, keepdims=True)
        - normed * jnp.mean(scaled * normed, axis=-1, keepdims=True)
    )


def mm_nn(left, right):
    return lax.dot_general(left, right, (((1,), (0,)), ((), ())), preferred_element_type=F32)


def mm_nt(left, right):
    return lax.dot_general(left, right, (((1,), (1,)), ((), ())), preferred_element_type=F32)


def mm_tn(left, right):
    return lax.dot_general(left, right, (((0,), (0,)), ((), ())), preferred_element_type=F32)


def column_sum(value):
    return jnp.sum(value, axis=0, keepdims=True)


def head_masks(cols, scale=1.0):
    lane = lax.broadcasted_iota(jnp.int32, (1, cols), 1)
    return [
        jnp.where((lane >= h * HD) & (lane < (h + 1) * HD), scale, 0.0).astype(BF16)
        for h in range(cols // HD)
    ]


def attend_kernel(
    place, x, gain, bias, w_qkv, bias_qv, w_out,
    nf, q, k, v, probs, mixed, part0, part1, part2, part3, part_all,
):
    t = place[0]
    images, seq, _ = x.shape
    rows = part0.shape[0]
    cols = q.shape[1]
    scaled_masks = head_masks(cols, HD ** (-0.5))
    masks = head_masks(cols)
    live_key = lax.broadcasted_iota(jnp.int32, (rows, rows), 1) < seq

    def image(r, carry):
        here = pl.ds(pl.multiple_of(r * rows, 16), rows)
        normed, _ = norm_stats(x[t ^ r].astype(F32))
        nf[pl.ds(pl.multiple_of(r * rows + rows - 16, 16), 16), :] = jnp.zeros((16, nf.shape[1]), BF16)
        nf[pl.ds(pl.multiple_of(r * rows, 16), seq), :] = (normed * gain[...] + bias[...]).astype(BF16)
        n = nf[here, :]
        q_here = (mm_nt(n, w_qkv[0]) + bias_qv[0:1, :]).astype(BF16)
        k_here = mm_nt(n, w_qkv[1]).astype(BF16)
        v_here = (mm_nt(n, w_qkv[2]) + bias_qv[1:2, :]).astype(BF16)
        q[here, :] = q_here
        k[here, :] = k_here
        v[here, :] = v_here
        total = jnp.zeros((rows, cols), F32)
        for h in range(cols // HD):
            scores = jnp.where(live_key, mm_nt(q_here * scaled_masks[h], k_here), -1e30)
            top = jnp.max(scores, axis=1, keepdims=True)
            weights = jnp.exp(scores - top)
            inverse = 1.0 / jnp.sum(weights, axis=1, keepdims=True)
            prob = (weights * inverse).astype(BF16)
            probs[h, here, :] = prob
            total = total + mm_nn(prob, v_here * masks[h])
        mixed_here = total.astype(BF16)
        mixed[here, :] = mixed_here
        part_all[r] = mm_nn(mixed_here, w_out[...]).astype(BF16)
        return carry

    lax.fori_loop(0, images, image, 0)
    for r, part in enumerate((part0, part1, part2, part3)):
        part[...] = part_all[r]


def second_norm_kernel(place, x, part0, recv1, recv2, bias_out, gain, bias, resid, norm):
    seq = x.shape[1]
    rows = resid.shape[0]
    proj = (part0[...].astype(F32) + recv1[...].astype(F32)) + recv2[...].astype(F32)
    resid[...] = proj + bias_out[...]
    resid[0:seq, :] = x[place[0]].astype(F32) + resid[0:seq, :]
    normed, _ = norm_stats(resid[...])
    live = lax.broadcasted_iota(jnp.int32, (rows, 1), 0) < seq
    norm[...] = jnp.where(live, normed * gain[...] + bias[...], 0.0).astype(BF16)


def feed_kernel(
    place, n0, n1, n2, n3, grad_out, w_up, bias_up, w_down,
    activ, grad_up, grad_rows, part0, part1, part2, part3, sums, part_all, n_all, up_all,
):
    t = place[0]
    images, seq, width = grad_out.shape
    rows = n0.shape[0]
    hidden = w_up.shape[1]
    for r, n in enumerate((n0, n1, n2, n3)):
        n_all[r] = n[...]
    sums[...] = jnp.zeros(sums.shape, F32)
    chunk = 256

    def image(r, carry):
        first = pl.multiple_of(r * rows, 16)
        here = pl.ds(first, rows)
        n = n_all[r]
        live = jnp.where((t ^ r) < place[1], 1.0, 0.0)
        grad_rows[pl.ds(pl.multiple_of(first + rows - 16, 16), 16), :] = jnp.zeros((16, width), BF16)
        grad_rows[pl.ds(first, seq), :] = (grad_out[t ^ r].astype(F32) * live).astype(BF16)
        g = grad_rows[here, :]
        sums[1:2, :] += column_sum(g.astype(F32))
        total = jnp.zeros((rows, width), F32)
        for c in range(0, hidden, chunk):
            part = slice(c, c + chunk)
            upper = mm_nn(n, w_up[:, part]) + bias_up[:, part]
            share = 0.5 * (1.0 + lax.erf(upper * SQRT_HALF))
            activ[here, part] = (upper * share).astype(BF16)
            slope = share + upper * jnp.exp(-0.5 * upper * upper) * INV_ROOT_TWO_PI
            grad = mm_nn(g, w_down[:, part]) * slope
            sums[0:1, part] += column_sum(grad)
            grad_b = grad.astype(BF16)
            grad_up[here, part] = grad_b
            total = total + mm_nt(grad_b, w_up[:, part])
        part_all[r] = total.astype(BF16)
        return carry

    lax.fori_loop(0, images, image, 0)
    for r, part in enumerate((part0, part1, part2, part3)):
        part[...] = part_all[r]


def feed_weights_kernel(n0, n1, n2, n3, activ, grad_up, grad_rows, grads, n_all):
    rows = n0.shape[0]
    width = n0.shape[1]
    for r, n in enumerate((n0, n1, n2, n3)):
        n_all[r * rows : (r + 1) * rows, :] = n[...]
    hidden = activ.shape[1]
    chunk = 256
    for c in range(0, width, chunk):
        part = slice(c, c + chunk)
        grads[part, 0:hidden] = mm_tn(grad_rows[:, part], activ[...]).astype(BF16)
        grads[part, hidden : 2 * hidden] = mm_tn(n_all[:, part], grad_up[...]).astype(BF16)


def feed_down_kernel(activ, w_down, part0, part1, part2, part3):
    rows = part0.shape[0]
    for r, part in enumerate((part0, part1, part2, part3)):
        part[...] = mm_nt(activ[r * rows : (r + 1) * rows, :], w_down[...]).astype(BF16)


def output_kernel(place, resid, part0, recv1, recv2, bias_down, out):
    live = jnp.where(place[0] < place[1], 1.0, 0.0)
    down = (part0[...].astype(F32) + recv1[...].astype(F32)) + recv2[...].astype(F32)
    out[...] = (live * (resid[...] + down + bias_down[...])).astype(BF16)


def middle_kernel(resid, grad_rows, part0, recv1, recv2, gain, grad_resid, grad_resid_b, sums):
    grad_norm = (part0[...].astype(F32) + recv1[...].astype(F32)) + recv2[...].astype(F32)
    normed, inverse = norm_stats(resid[...])
    grad = grad_rows[...].astype(F32) + norm_back(grad_norm, gain[...], normed, inverse)
    grad_resid[...] = grad
    grad_resid_b[...] = grad.astype(BF16)
    sums[0:1, :] = column_sum(grad)
    sums[1:2, :] = column_sum(grad_norm * normed)
    sums[2:3, :] = column_sum(grad_norm)
    sums[3:8, :] = jnp.zeros((5, sums.shape[1]), F32)


def attend_back_kernel(
    g0, g1, g2, g3, q, k, v, probs, nf, w_qkv, w_out, gain, bias,
    grad_qkv, part0, part1, part2, part3, sums, sums_qv, part_all, g_all,
):
    rows = g0.shape[0]
    cols = q.shape[1]
    scale = HD ** (-0.5)
    masks = head_masks(cols)
    for r, g in enumerate((g0, g1, g2, g3)):
        g_all[r] = g[...]
    sums[...] = jnp.zeros(sums.shape, F32)
    sums_qv[...] = jnp.zeros(sums_qv.shape, F32)

    def image(r, carry):
        here = pl.ds(pl.multiple_of(r * rows, 16), rows)
        grad_mixed = mm_nt(g_all[r], w_out[...]).astype(BF16)
        q_here = q[here, :]
        k_here = k[here, :]
        v_here = v[here, :]
        grad_q = jnp.zeros((rows, cols), F32)
        grad_k = jnp.zeros((rows, cols), F32)
        grad_v = jnp.zeros((rows, cols), F32)
        for h in range(cols // HD):
            prob_b = probs[h, here, :]
            prob = prob_b.astype(F32)
            grad_mixed_h = grad_mixed * masks[h]
            grad_prob = mm_nt(grad_mixed_h, v_here)
            delta = jnp.sum(prob * grad_prob, axis=1, keepdims=True)
            grad_score = (prob * (grad_prob - delta) * scale).astype(BF16)
            grad_q = grad_q + mm_nn(grad_score, k_here * masks[h])
            grad_k = grad_k + mm_tn(grad_score, q_here * masks[h])
            grad_v = grad_v + mm_tn(prob_b, grad_mixed_h)
        sums_qv[0:1, :] += column_sum(grad_q)
        sums_qv[1:2, :] += column_sum(grad_v)
        total = jnp.zeros((rows, nf.shape[1]), F32)
        for c, grad in enumerate((grad_q, grad_k, grad_v)):
            grad_b = grad.astype(BF16)
            grad_qkv[c, here, :] = grad_b
            total = total + mm_nn(grad_b, w_qkv[c])
        part_all[r] = total.astype(BF16)
        sums[0:1, :] += column_sum(total * nf[here, :].astype(F32))
        sums[1:2, :] += column_sum(total)
        return carry

    lax.fori_loop(0, g_all.shape[0], image, 0)
    sums[0:1, :] = (sums[0:1, :] - bias[...] * sums[1:2, :]) / gain[...]
    for r, part in enumerate((part0, part1, part2, part3)):
        part[...] = part_all[r]


def attend_weights_kernel(g0, g1, g2, g3, mixed, nf, grad_qkv, grads, g_all):
    rows = g0.shape[0]
    width = g0.shape[1]
    cols = mixed.shape[1]
    for r, g in enumerate((g0, g1, g2, g3)):
        g_all[r * rows : (r + 1) * rows, :] = g[...]
    chunk = 256
    for c in range(0, width, chunk):
        part = slice(c, c + chunk)
        grads[part, 0:cols] = mm_tn(g_all[:, part], mixed[...]).astype(BF16)
        for i in range(3):
            lanes = slice((i + 1) * cols, (i + 2) * cols)
            grads[part, lanes] = mm_tn(nf[:, part], grad_qkv[i]).astype(BF16)


def input_grad_kernel(place, x, grad_resid, part0, recv1, recv2, gain, out):
    seq = x.shape[1]
    out[seq // 16 * 16 :, :] = jnp.zeros((out.shape[0] - seq // 16 * 16, out.shape[1]), BF16)
    own = slice(0, seq)
    grad_norm = part0[own, :].astype(F32) + recv1[own, :].astype(F32) + recv2[own, :].astype(F32)
    normed, inverse = norm_stats(x[place[0]].astype(F32))
    grad = grad_resid[own, :] + norm_back(grad_norm, gain[...], normed, inverse)
    out[own, :] = grad.astype(BF16)


def assemble_kernel(place, r0, r1, r2, r3, out):
    seq = out.shape[1]
    for r, value in enumerate((r0, r1, r2, r3)):
        out[place[0] ^ r] = value[0:seq, :]


def call(kernel, outs, args, place=None, scratch=(), flops=0):
    in_specs = [pl.BlockSpec(memory_space=pltpu.VMEM) for _ in args]
    if place is not None:
        in_specs = [pl.BlockSpec(memory_space=pltpu.SMEM)] + in_specs
        args = (place,) + tuple(args)
    moved = sum(math.prod(a.shape) * a.dtype.itemsize for a in tuple(args) + tuple(outs))
    single = len(outs) == 1
    return pl.pallas_call(
        kernel,
        out_shape=outs[0] if single else tuple(outs),
        in_specs=in_specs,
        out_specs=jax.tree.map(
            lambda _: pl.BlockSpec(memory_space=pltpu.VMEM), outs[0] if single else tuple(outs)
        ),
        scratch_shapes=list(scratch),
        compiler_params=pltpu.CompilerParams(vmem_limit_bytes=48 * 2**20),
        cost_estimate=pl.CostEstimate(
            flops=int(flops), bytes_accessed=int(moved), transcendentals=0
        ),
    )(*args)


def shaped(shape, dtype):
    return jax.ShapeDtypeStruct(tuple(shape), dtype)


def swap(value, axis, bit):
    size = lax.axis_size(axis)
    return lax.ppermute(value, axis, [(i, i ^ bit) for i in range(size)])


def add_b(left, right):
    return (left.astype(F32) + right.astype(F32)).astype(BF16)


def tensor_scatter(parts):
    recv3 = swap(parts[3], "tensor", 1)
    recv1 = swap(parts[1], "tensor", 1)
    recv2 = swap(add_b(parts[2], recv3), "tensor", 2)
    return parts[0], recv1, recv2


def tensor_gather(own):
    recv2 = swap(own, "tensor", 2)
    recv1 = swap(own, "tensor", 1)
    recv3 = swap(recv2, "tensor", 1)
    return own, recv1, recv2, recv3


def group_bits():
    return lax.axis_size("dp").bit_length() - 1


def group_scatter(value):
    size = lax.axis_size("dp")
    me = lax.axis_index("dp")
    held = value.reshape(size, value.shape[0] // size, value.shape[1])
    for b in range(group_bits()):
        bit = (me >> b) & 1
        pairs = held.reshape(held.shape[0] // 2, 2, held.shape[1], held.shape[2])
        keep = lax.dynamic_index_in_dim(pairs, bit, 1, keepdims=False)
        send = lax.dynamic_index_in_dim(pairs, 1 - bit, 1, keepdims=False)
        recv = swap(send.astype(BF16), "dp", 1 << b)
        held = keep.astype(F32) + recv.astype(F32)
    return held[0]


def summed_over(value, axis):
    for b in range(lax.axis_size(axis).bit_length() - 1):
        value = value + swap(value, axis, 1 << b)
    return value


def per_device(
    layer_input,
    group_images,
    ln1_gain,
    ln1_bias,
    w_qkv,
    bias_qv,
    w_out,
    bias_out,
    ln2_gain,
    ln2_bias,
    w_up,
    bias_up,
    w_down,
    bias_down,
    grad_out,
):
    images, seq, width = layer_input.shape
    cols = w_qkv.shape[2]
    hidden = w_up.shape[1]
    heads = cols // HD
    rows = -(-seq // 16) * 16
    every = images * rows
    place = jnp.stack([lax.axis_index("tensor").astype(jnp.int32), group_images[0]])
    w_qkv_t = w_qkv.transpose(1, 2, 0)
    w_out_t = w_out.T
    as_row = lambda value: value.reshape(1, -1)
    block = shaped((rows, width), BF16)
    block32 = shaped((rows, width), F32)
    stacked = pltpu.VMEM((images, rows, width), BF16)
    flat = pltpu.VMEM((every, width), BF16)
    dense = 2 * every * width

    nf, q, k, v, probs, mixed, *parts = call(
        attend_kernel,
        [shaped((every, width), BF16)]
        + [shaped((every, cols), BF16)] * 3
        + [shaped((heads, every, rows), BF16), shaped((every, cols), BF16)]
        + [block] * 4,
        (layer_input, as_row(ln1_gain), as_row(ln1_bias), w_qkv_t, bias_qv.T, w_out_t),
        place,
        [stacked],
        flops=dense * cols * 4,
    )
    resid, norm_own = call(
        second_norm_kernel,
        [block32, block],
        (layer_input, *tensor_scatter(parts), as_row(bias_out), as_row(ln2_gain), as_row(ln2_bias)),
        place,
    )
    norms = tensor_gather(norm_own)
    activ, grad_up, grad_rows, *parts = call(
        feed_kernel,
        [shaped((every, hidden), BF16)] * 2
        + [shaped((every, width), BF16)]
        + [block] * 4
        + [shaped((8, width), F32)],
        (*norms, grad_out, w_up, as_row(bias_up), w_down),
        place,
        [stacked, stacked, pltpu.VMEM((rows, width), F32)],
        flops=dense * hidden * 3,
    )
    feed_sums = parts.pop()
    terms = tensor_scatter(parts)
    feed_grads = call(
        feed_weights_kernel,
        [shaped((width, 2 * hidden), BF16)],
        (*norms, activ, grad_up, grad_rows),
        None,
        [flat],
        flops=dense * hidden * 2,
    )
    down_parts = call(
        feed_down_kernel, [block] * 4, (activ, w_down), flops=dense * hidden
    )
    grad_resid, resid_b, middle_sums = call(
        middle_kernel,
        [block32, block, shaped((8, width), F32)],
        (resid, grad_rows[0:rows], *terms, as_row(ln2_gain)),
    )
    grads_b = tensor_gather(resid_b)
    output_own = call(
        output_kernel, [block], (resid, *tensor_scatter(down_parts), as_row(bias_down)), place
    )
    outputs = tensor_gather(output_own)
    grad_qkv, *parts = call(
        attend_back_kernel,
        [shaped((3, every, cols), BF16)]
        + [block] * 4
        + [shaped((8, width), F32), shaped((8, cols), F32)],
        (*grads_b, q, k, v, probs, nf, w_qkv_t, w_out_t, as_row(ln1_gain), as_row(ln1_bias)),
        None,
        [stacked, stacked],
        flops=dense * cols * 5,
    )
    sums_qv = parts.pop()
    first_sums = parts.pop()
    terms = tensor_scatter(parts)
    attend_grads = call(
        attend_weights_kernel,
        [shaped((width, 4 * cols), BF16)],
        (*grads_b, mixed, nf, grad_qkv),
        None,
        [flat],
        flops=dense * cols * 4,
    )
    shared = summed_over(jnp.concatenate([first_sums[0:2], middle_sums[0:3]]), "tensor")
    small = jnp.concatenate(
        [shared, feed_sums[0:2], jnp.pad(sums_qv[0:2], ((0, 0), (0, width - cols)))]
    )
    small = summed_over(small, "dp")
    attend_sum = group_scatter(attend_grads)
    feed_sum = group_scatter(feed_grads)
    grad_in_own = call(
        input_grad_kernel, [block], (layer_input, grad_resid, *terms, as_row(ln1_gain)), place
    )
    grad_ins = tensor_gather(grad_in_own)
    output = call(assemble_kernel, [shaped(layer_input.shape, BF16)], outputs, place)
    grad_input = call(assemble_kernel, [shaped(layer_input.shape, BF16)], grad_ins, place)

    share = width // lax.axis_size("dp")
    me = lax.axis_index("dp")
    own = lax.dynamic_slice_in_dim(small, me * share, share, 1)
    share_up = hidden // lax.axis_size("dp")
    own_up = lax.dynamic_slice_in_dim(small[5], me * share_up, share_up, 0)
    share_qv = cols // lax.axis_size("dp")
    own_qv = lax.dynamic_slice_in_dim(small[7:9, 0:cols], me * share_qv, share_qv, 1)
    grad_w_qkv = attend_sum[:, cols:].reshape(share, 3, cols)
    return (
        output,
        grad_input,
        own[0],
        own[1],
        grad_w_qkv,
        own_qv.T,
        attend_sum[:, 0:cols],
        own[2],
        own[3],
        own[4],
        feed_sum[:, hidden:],
        own_up,
        feed_sum[:, 0:hidden],
        own[6],
    )


def solution(mesh):
    placed = (
        P("dp", None, None),
        P("dp"),
        P(),
        P(),
        P(None, None, "tensor"),
        P("tensor", None),
        P(None, "tensor"),
        P(),
        P(),
        P(),
        P(None, "tensor"),
        P("tensor"),
        P(None, "tensor"),
        P(),
        P("dp", None, None),
    )
    return jax.shard_map(
        per_device,
        mesh=mesh,
        in_specs=placed,
        out_specs=(
            P("dp", None, None),
            P("dp", None, None),
            P("dp"),
            P("dp"),
            P("dp", None, "tensor"),
            P(("tensor", "dp"), None),
            P("dp", "tensor"),
            P("dp"),
            P("dp"),
            P("dp"),
            P("dp", "tensor"),
            P(("tensor", "dp")),
            P("dp", "tensor"),
            P("dp"),
        ),
        check_vma=False,
    )
```
